32 devices in a mesh: seq: 8 (over z, x), tp: 4 (over y, core).
Axes of the slice: x: 2, y: 2, z: 4, core: 2. Of those that a mesh axis runs over, the one named last changes fastest.
Arguments:
- hidden_new: bfloat16 [3, 16, 8192], P(None, None, 'seq'), may hold values from -6 to 6
- w_kv: bfloat16 [8192, 8, 256], P('seq', 'tp'), may hold values from -0.0625 to 0.0625
- w_out: bfloat16 [8192, 8192], P('tp', 'seq'), may hold values from -0.0625 to 0.0625
- queries_draft: bfloat16 [3, 4, 8, 32, 128], P(None, None, 'tp'), may hold values from -48 to 48
- queries_verify: bfloat16 [3, 4, 8, 32, 128], P(None, None, 'tp'), may hold values from -48 to 48
- keys_cache: bfloat16 [4, 8, 16384, 128], P(None, 'tp', 'seq'), may hold values from -6 to 6
- values_cache: bfloat16 [4, 8, 16384, 128], P(None, 'tp', 'seq'), may hold values from -6 to 6
- key_levels: bfloat16 [4, 8, 16384, 128], P(None, 'tp', 'seq'), may hold values from -8 to 7, as said below
- value_levels: bfloat16 [4, 8, 16384, 128], P(None, 'tp', 'seq'), may hold values from -8 to 7, as said below
- key_scales: float32 [4, 8, 16384], P(None, 'tp', 'seq'), may hold values from 0.05 to 0.5
- value_scales: float32 [4, 8, 16384], P(None, 'tp', 'seq'), may hold values from 0.1 to 0.4
- lengths: int32 [4], replicated, may hold values from 2 to 16376, as said below
- accepted: int32 [2, 4], replicated, may hold values from 0 to 4, as said below
Outputs:
- layer_out: bfloat16 [3, 2, 16, 8192], P(None, None, None, 'seq')
The draws below stay inside these ranges and needn't reach their ends.
Inputs may be any that keep to these rules, and one draw needn't show every extreme that they name: `key_levels`: every entry is a whole number. Positions 0 and 1 of every sequence and head hold equal levels. `value_levels`: every entry is a whole number. `lengths`: some sequence starts with exactly 16376 valid positions, another with 16 or fewer. `accepted`: the values 0 and 4 both occur.
All inputs are finite; a program needn't handle non-finite values.
Results may differ from the reference program's by a relative error of at most 0.006.
The reference program's roundings to bfloat16 on the way count: a program that leaves them out, or rounds other values in their place, can miss the bound.
Values may be sent and summed in bfloat16 or wider, within the bound.
A program may use at most 128 MiB of HBM per device.

```python
import math
import jax
import jax.numpy as jnp
from jax import lax

D = 8192
KVH = 8
HD = 128
GROUP = 8
B = 4
S_DEV = 2048
R = 4
ROUNDS = 3
CTX = 16384
N_SEQ = 8


def first_levels(key):
    return jax.random.randint(jax.random.fold_in(key, 902), (B, KVH, HD), -8, 8, dtype=jnp.int32).astype(jnp.float32)


def broad_rows(key, label, base_rows):
    shape_full = (ROUNDS, B, KVH, GROUP * R, HD)
    chosen = jax.random.randint(jax.random.fold_in(key, label), (ROUNDS, B, KVH, GROUP * R), 0, 8) == 0
    signs = jnp.where(jax.random.bernoulli(jax.random.fold_in(key, label + 1), 0.5, shape_full), 1.0, -1.0)
    magnitude = jax.random.uniform(jax.random.fold_in(key, label + 2), shape_full, jnp.float32, 24.0, 48.0)
    return jnp.where(chosen[..., None], signs * magnitude, base_rows)


def draw_queries_draft(key, part):
    base_rows = jnp.clip(3.0 * jax.random.normal(jax.random.fold_in(key, 31), (ROUNDS, B, KVH, GROUP * R, HD), jnp.float32), -12.0, 12.0)
    base_rows = broad_rows(key, 71, base_rows)
    return base_rows.astype(jnp.bfloat16)


def draw_queries_verify(key, part):
    base_rows = jnp.clip(3.0 * jax.random.normal(jax.random.fold_in(key, 32), (ROUNDS, B, KVH, GROUP * R, HD), jnp.float32), -12.0, 12.0)
    base_rows = broad_rows(key, 81, base_rows)
    return base_rows.astype(jnp.bfloat16)


def draw_keys_cache(key, part):
    base_rows = jnp.clip(jax.random.normal(jax.random.fold_in(key, 33), (B, KVH, CTX, HD), jnp.float32), -6.0, 6.0)
    return base_rows.astype(jnp.bfloat16)


def draw_key_scales(key, part):
    uniform_log = jax.random.uniform(jax.random.fold_in(key, 34), (B, KVH, CTX), jnp.float32)
    scales = jnp.exp(math.log(0.15) + uniform_log * (math.log(0.3) - math.log(0.15)))
    return scales


def draw_key_levels(key, part):
    levels = jax.random.randint(jax.random.fold_in(key, 61), (B, KVH, CTX, HD), -8, 8, dtype=jnp.int32).astype(jnp.float32)
    leading = first_levels(key)
    levels = levels.at[:, :, 0, :].set(leading).at[:, :, 1, :].set(leading)
    return levels.astype(jnp.bfloat16)


def draw_value_levels(key, part):
    levels = jax.random.randint(jax.random.fold_in(key, 62), (B, KVH, CTX, HD), -8, 8, dtype=jnp.int32).astype(jnp.float32)
    return levels.astype(jnp.bfloat16)


def draw_lengths(key, part):
    longest = CTX - (ROUNDS - 1) * R
    top_bits = max(longest.bit_length() - 1, 1)
    exponents = jax.random.randint(jax.random.fold_in(key, 51), (B,), 1, top_bits + 1, dtype=jnp.int32)
    lowest = jnp.left_shift(jnp.ones((B,), jnp.int32), exponents)
    values_drawn = jax.random.randint(jax.random.fold_in(key, 52), (B,), lowest, 2 * lowest, dtype=jnp.int32)
    values_drawn = jnp.clip(values_drawn, 2, longest)
    picked = jax.random.randint(jax.random.fold_in(key, 55), (), 0, B, dtype=jnp.int32)
    other = (picked + jax.random.randint(jax.random.fold_in(key, 56), (), 1, B, dtype=jnp.int32)) % B
    short_len = jax.random.randint(jax.random.fold_in(key, 57), (), 2, min(17, longest + 1), dtype=jnp.int32)
    return values_drawn.at[picked].set(longest).at[other].set(short_len).astype(jnp.int32)


def draw_accepted(key, part):
    counts = jax.random.randint(jax.random.fold_in(key, 53), ((ROUNDS - 1) * B,), 0, R + 1, dtype=jnp.int32)
    picked = jax.random.permutation(jax.random.fold_in(key, 54), (ROUNDS - 1) * B)
    counts = counts.at[picked[0]].set(R).at[picked[1]].set(0)
    return counts.reshape(ROUNDS - 1, B).astype(jnp.int32)


def block_scale(rng, shape, pieces, least, top_value):
    loudness = 1.0
    for dim, blocks in pieces:
        steps = jax.random.uniform(jax.random.fold_in(jax.random.fold_in(rng, 6), dim), (blocks,), jnp.float32, least / len(pieces), top_value / len(pieces))
        loudness = loudness * jnp.repeat(jnp.exp(steps), shape[dim] // blocks).reshape((-1,) + (1,) * (len(shape) - 1 - dim))
    return loudness


def scatter_about(stream_key, shape, width, limit, split=(), held_as=jnp.bfloat16):
    result = jax.random.normal(stream_key, shape, jnp.float32) * width
    if len(split) > 0:
        result = block_scale(stream_key, shape, split, -0.22, 0.18) * result
    return jnp.clip(result, min=-limit, max=limit).astype(held_as)


def setup_inputs(seed: int = 0) -> dict:
    arg_keys = jax.random.split(jax.random.key(seed), 14)
    return {
        "hidden_new": scatter_about(arg_keys[0], (ROUNDS, B * R, D), 1.0, 6.0, ((2, 8),)),
        "w_kv": scatter_about(arg_keys[1], (D, KVH, 2 * HD), D ** -0.5, 0.0625, ((0, 8), (1, 4))),
        "w_out": scatter_about(arg_keys[2], (KVH * GROUP * HD, D), (KVH * GROUP * HD) ** -0.5, 0.0625, ((0, 4), (1, 8))),
        "queries_draft": draw_queries_draft(jax.random.fold_in(arg_keys[13], 71), 0),
        "queries_verify": draw_queries_verify(jax.random.fold_in(arg_keys[13], 71), 0),
        "keys_cache": draw_keys_cache(jax.random.fold_in(arg_keys[13], 71), 0),
        "values_cache": scatter_about(arg_keys[6], (B, KVH, CTX, HD), 1.0, 6.0, ((1, 4), (2, 8))),
        "key_levels": draw_key_levels(jax.random.fold_in(arg_keys[13], 71), 0),
        "value_levels": draw_value_levels(jax.random.fold_in(arg_keys[13], 71), 0),
        "key_scales": draw_key_scales(jax.random.fold_in(arg_keys[13], 71), 0),
        "value_scales": jnp.clip(jnp.exp(math.log(0.4) - 1.3862944 * jax.random.uniform(arg_keys[10], (B, KVH, CTX), jnp.float32) ** block_scale(arg_keys[10], (B, KVH, CTX), ((1, 4), (2, 8)), -0.2, 0.2)), 0.1, 0.4),
        "lengths": draw_lengths(jax.random.fold_in(arg_keys[13], 71), 0),
        "accepted": draw_accepted(jax.random.fold_in(arg_keys[13], 71), 0),
    }


NEG = -1e+30

def dequantize(levels, scales):
    return (levels.astype(jnp.float32) * scales[..., None]).astype(jnp.bfloat16)

def attend(queries, keys, values, usable):
    scores = jnp.einsum('bhqd,bhkd->bhqk', queries.astype(jnp.float32), keys.astype(jnp.float32)) * (1.0 / math.sqrt(HD))
    scores = jnp.where(usable, scores, NEG)
    maxima = lax.optimization_barrier(jnp.max(scores, axis=-1))
    weights = jnp.where(usable, jnp.exp(scores - maxima[..., None]), 0.0).astype(jnp.bfloat16)
    totals = lax.optimization_barrier(jnp.sum(weights.astype(jnp.float32), axis=-1))
    weighted = jnp.einsum('bhqk,bhkd->bhqd', weights.astype(jnp.float32), values.astype(jnp.float32))
    return (maxima, totals, weighted)

def combine(former, latter):
    highest = jnp.maximum(former[0], latter[0])
    former_w = jnp.exp(former[0] - highest)
    latter_w = jnp.exp(latter[0] - highest)
    return (highest, former[1] * former_w + latter[1] * latter_w, former[2] * former_w[..., None] + latter[2] * latter_w[..., None])

def finish(partial_value):
    return (partial_value[2] / partial_value[1][..., None]).astype(jnp.bfloat16)

def arrange(attended):
    return attended.reshape(2, B, KVH, GROUP, R, HD).transpose(0, 1, 4, 2, 3, 5).reshape(2 * B * R, KVH * GROUP * HD)

def reference(hidden_new, w_kv, w_out, queries_draft, queries_verify, keys_cache, values_cache, key_levels, value_levels, key_scales, value_scales, lengths, accepted):
    flat_kv = w_kv.reshape(D, KVH * 2 * HD)
    tokens = jnp.arange(GROUP * R, dtype=jnp.int32) % R
    causal = (tokens[:, None] >= jnp.arange(R, dtype=jnp.int32)[None, :])[None, None]
    offsets = jnp.arange(R, dtype=jnp.int32)[None, :]
    batch_rows = jnp.broadcast_to(jnp.arange(B, dtype=jnp.int32)[:, None], (B, R))
    blocks = jnp.arange(N_SEQ, dtype=jnp.int32)
    length_now = lengths
    results = []
    for turn_index in range(ROUNDS):
        fresh_rows = jnp.dot(hidden_new[turn_index], flat_kv, preferred_element_type=jnp.float32).astype(jnp.bfloat16).reshape(B, R, KVH, 2, HD)
        new_keys = fresh_rows[:, :, :, 0].transpose(0, 2, 1, 3)
        new_values = fresh_rows[:, :, :, 1].transpose(0, 2, 1, 3)
        draft_q = queries_draft[turn_index]
        verify_q = queries_verify[turn_index]

        def visit(running, block_index):
            first_row = block_index * S_DEV
            key_rows = lax.dynamic_slice_in_dim(keys_cache, first_row, S_DEV, 2)
            value_rows = lax.dynamic_slice_in_dim(values_cache, first_row, S_DEV, 2)
            key_low = dequantize(lax.dynamic_slice_in_dim(key_levels, first_row, S_DEV, 2), lax.dynamic_slice_in_dim(key_scales, first_row, S_DEV, 2))
            value_low = dequantize(lax.dynamic_slice_in_dim(value_levels, first_row, S_DEV, 2), lax.dynamic_slice_in_dim(value_scales, first_row, S_DEV, 2))
            places = first_row + jnp.arange(S_DEV, dtype=jnp.int32)
            stored = (places[None, :] < lengths[:, None])[:, None, :, None]
            usable = (places[None, :] < length_now[:, None])[:, None, None, :]
            draft_keys = jnp.where(stored, key_low, key_rows)
            draft_values = jnp.where(stored, value_low, value_rows)
            draft_part = attend(draft_q, draft_keys, draft_values, usable)
            verify_part = attend(verify_q, key_rows, value_rows, usable)
            return ((combine(running[0], draft_part), combine(running[1], verify_part)), None)
        initial = (jnp.full((B, KVH, GROUP * R), NEG, jnp.float32), jnp.zeros((B, KVH, GROUP * R), jnp.float32), jnp.zeros((B, KVH, GROUP * R, HD), jnp.float32))
        merged, unused = lax.scan(visit, (initial, initial), blocks)
        draft_all = combine(merged[0], attend(draft_q, new_keys, new_values, causal))
        verify_all = combine(merged[1], attend(verify_q, new_keys, new_values, causal))
        attended = jnp.stack([finish(draft_all), finish(verify_all)])
        projected = jnp.dot(arrange(attended), w_out, preferred_element_type=jnp.float32)
        results.append(projected.astype(jnp.bfloat16).reshape(2, B * R, D))
        if turn_index + 1 < ROUNDS:
            accepted_now = accepted[turn_index]
            places = jnp.where(offsets < accepted_now[:, None], length_now[:, None] + offsets, CTX)
            keys_cache = keys_cache.at[batch_rows, :, places, :].set(fresh_rows[:, :, :, 0], mode='drop')
            values_cache = values_cache.at[batch_rows, :, places, :].set(fresh_rows[:, :, :, 1], mode='drop')
            length_now = length_now + accepted_now
    return jnp.stack(results)
```

```python
import functools
import math

import jax
import jax.numpy as jnp
from jax import lax
from jax.experimental import pallas as pl
from jax.experimental.pallas import tpu as pltpu
from jax.sharding import PartitionSpec as P

NEG = -1e30
LANES = 128
F32 = jnp.float32
BF16 = jnp.bfloat16


def onehot(rows, cols, source):
    r = lax.broadcasted_iota(jnp.int32, (rows, cols), 0)
    c = lax.broadcasted_iota(jnp.int32, (rows, cols), 1)
    return (source(r) == c).astype(F32).astype(BF16)


def kernel(cfg, *refs):
    (len_s, acc_s, hid_v, sc_v, qd_v, qv_v, wkv_h, wout_h, k_h, v_h, kl_h, vl_h, out_ref,
     wkv, wout, kc, vc, kl, vl, lowk, lowv, scores,
     fr_send, fr_recv, o_send, o_recv, st_send, st_recv, ag, amat, rs_send, rs_recv, fin,
     in_sem, kv_sem, frs_sem, frr_sem, os_sem, or_sem, ss_sem, sr_sem,
     ags_sem, agf_sem, agr_sem, rss_sem, rsr_sem, fs_sem, ffr_sem) = refs
    n, tp, batch, heads, rounds, R, group, S, HD, split_cols = cfg
    pairs = batch * heads
    k = n // pairs
    rows1 = rounds * group * R
    rows = 2 * rows1
    fpad = fr_send.shape[1]
    pad_rows = st_send.shape[2]
    me = lax.axis_index("seq")
    tpi = lax.axis_index("tp")
    mine = lax.div(me, k)
    sub = lax.rem(me, k)
    MESH = pl.DeviceIdType.MESH

    cp_wkv = pltpu.make_async_copy(wkv_h, wkv, in_sem.at[0])
    cp_wkv.start()
    cp_wout = pltpu.make_async_copy(wout_h, wout, in_sem.at[1])

    def cache_copies(p):
        b = lax.div(p, heads)
        h = lax.rem(p, heads)
        return [
            pltpu.make_async_copy(src.at[b, h], dst.at[p], kv_sem.at[j, p])
            for j, (src, dst) in enumerate(((kl_h, kl), (k_h, kc), (vl_h, vl), (v_h, vc)))
        ]

    for step in range(1, pairs + 1):
        for c in cache_copies(lax.rem(mine + step, pairs)):
            c.start()
    cp_wout.start()

    barrier = pltpu.get_barrier_semaphore()
    for j in range(1, n):
        pl.semaphore_signal(barrier, inc=1, device_id={"seq": lax.rem(me + j, n)}, device_id_type=MESH)
    for j in range(1, tp):
        pl.semaphore_signal(barrier, inc=1, device_id={"tp": lax.rem(tpi + j, tp)}, device_id_type=MESH)

    tok = rounds * batch * R

    def fresh_source(r):
        b, q = r // fpad, r % fpad
        return jnp.where(q < rounds * R, (q // R) * (batch * R) + b * R + q % R, tok)

    hid = jnp.dot(onehot(batch * fpad, tok, fresh_source), hid_v[...], preferred_element_type=F32).astype(BF16)
    cp_wkv.wait()
    partial = jnp.dot(hid, wkv[...], preferred_element_type=F32)
    for p in range(pairs):
        b, h = p // heads, p % heads
        fr_send[p] = partial[b * fpad:(b + 1) * fpad, h * 2 * HD:(h + 1) * 2 * HD]
    pl.semaphore_wait(barrier, n - 1 + tp - 1)

    def fresh_copy(dst, slot):
        return pltpu.make_async_remote_copy(
            src_ref=fr_send.at[lax.div(dst, k)], dst_ref=fr_recv.at[slot],
            send_sem=frs_sem.at[dst], recv_sem=frr_sem.at[slot],
            device_id={"seq": dst}, device_id_type=MESH)

    for j in range(1, n):
        fresh_copy(lax.rem(me + j, n), me).start()
    fr_recv[me] = fr_send[mine]

    factor = (1.0 / math.sqrt(HD)) * math.log2(math.e)
    nch = S // LANES
    eye = (lax.broadcasted_iota(jnp.int32, (LANES, LANES), 0)
           == lax.broadcasted_iota(jnp.int32, (LANES, LANES), 1))
    spot = lax.broadcasted_iota(jnp.int32, (1, S), 1)

    def to_row(col):
        parts = []
        for c in range(pad_rows // LANES):
            lo, hi = c * LANES, min((c + 1) * LANES, rows)
            piece = jnp.where(eye[: hi - lo], col[lo:hi], 0.0)
            parts.append(jnp.sum(piece, axis=0, keepdims=True))
        return jnp.concatenate(parts, axis=1)

    def to_col(row):
        parts = []
        for c in range(pad_rows // LANES):
            lo, hi = c * LANES, min((c + 1) * LANES, rows)
            piece = jnp.where(eye[: hi - lo], row[:, lo:lo + LANES], 0.0)
            parts.append(jnp.sum(piece, axis=1, keepdims=True))
        return jnp.concatenate(parts, axis=0)

    def one_kind(q, keys, values, usable):
        s = lax.dot_general(q, keys, (((1,), (1,)), ((), ())), preferred_element_type=F32)
        s = jnp.where(usable, s * factor, NEG)
        m = jnp.max(s, axis=1, keepdims=True)
        w = jnp.where(usable, jnp.exp2(s - m), 0.0).astype(BF16)
        l = jnp.sum(w.astype(F32), axis=1, keepdims=True)
        o = jnp.dot(w, values, preferred_element_type=F32)
        return m, l, o

    def o_copy(p, dst, slot, src):
        return pltpu.make_async_remote_copy(
            src_ref=src, dst_ref=o_recv.at[slot], send_sem=os_sem.at[dst], recv_sem=or_sem.at[slot],
            device_id={"seq": dst}, device_id_type=MESH)

    def s_copy(p, dst, slot, src):
        return pltpu.make_async_remote_copy(
            src_ref=src, dst_ref=st_recv.at[slot], send_sem=ss_sem.at[dst], recv_sem=sr_sem.at[slot],
            device_id={"seq": dst}, device_id_type=MESH)

    def pair_part(p, o_dst, st_dst):
        b = lax.div(p, heads)
        h = lax.rem(p, heads)
        for c in cache_copies(p):
            c.wait()
        scales = sc_v[p].T
        for c in range(nch):
            sl = slice(c * LANES, (c + 1) * LANES)
            lowk[sl] = (kl[p, sl].astype(F32) * scales[:, c:c + 1]).astype(BF16)
            lowv[sl] = (vl[p, sl].astype(F32) * scales[:, nch + c:nch + c + 1]).astype(BF16)
        usable = (spot + me * S) < len_s[b]
        parts = [
            one_kind(qd_v[:, b, h].reshape(rows1, HD), lowk[...], lowv[...], usable),
            one_kind(qv_v[:, b, h].reshape(rows1, HD), kc[p], vc[p], usable),
        ]
        lses = []
        for j, (m, l, o) in enumerate(parts):
            some = l > 0.0
            safe = jnp.where(some, l, 1.0)
            o_dst[j * rows1:(j + 1) * rows1] = (o / safe).astype(BF16)
            lses.append(jnp.where(some, m + jnp.log2(safe), NEG))
        st_dst[...] = jnp.broadcast_to(to_row(jnp.concatenate(lses, axis=0)), st_dst.shape)

    @pl.loop(1, pairs)
    def _(step):
        p = lax.rem(mine + step, pairs)
        pair_part(p, o_send.at[p], st_send.at[p])
        for e in range(k):
            dst = p * k + lax.rem(sub + e, k)
            o_copy(p, dst, me, o_send.at[p]).start()
            s_copy(p, dst, me, st_send.at[p]).start()

    pair_part(mine, o_recv.at[me], st_recv.at[me])
    for e in range(1, k):
        dst = mine * k + lax.rem(sub + e, k)
        o_copy(mine, dst, me, o_recv.at[me]).start()
        s_copy(mine, dst, me, st_recv.at[me]).start()

    for j in range(1, n):
        fresh_copy(lax.rem(me + j, n), lax.rem(me + j, n)).wait_recv()
    total = fr_recv[0]
    for j in range(1, n):
        total = total + fr_recv[j]
    new_k = total[:, :HD].astype(BF16)
    new_v = total[:, HD:].astype(BF16)
    bm = lax.div(mine, heads)
    hm = lax.rem(mine, heads)
    r_id = lax.broadcasted_iota(jnp.int32, (rows1, fpad), 0)
    c_id = lax.broadcasted_iota(jnp.int32, (rows1, fpad), 1)
    turn, i_q = r_id // (group * R), r_id % R
    c_turn, c_j = c_id // R, c_id % R
    limit = jnp.zeros((rows1, fpad), jnp.int32)
    for t in range(rounds - 1):
        limit = jnp.where(c_turn == t, acc_s[t, bm], limit)
    see = ((c_turn < turn) & (c_j < limit)) | ((c_turn == turn) & (c_j <= i_q))
    dpart = one_kind(qd_v[:, bm, hm].reshape(rows1, HD), new_k, new_v, see)
    vpart = one_kind(qv_v[:, bm, hm].reshape(rows1, HD), new_k, new_v, see)
    M, L, O = (jnp.concatenate([a, b], axis=0) for a, b in zip(dpart, vpart))
    for j in range(n):
        src = lax.rem(me + j, n)
        if j:
            o_copy(mine, src, src, o_send.at[0]).wait_recv()
            s_copy(mine, src, src, st_send.at[0]).wait_recv()
        lse = to_col(st_recv[src][0:1])
        top = jnp.maximum(M, lse)
        wa = jnp.exp2(M - top)
        wb = jnp.where(lse > 0.5 * NEG, jnp.exp2(lse - top), 0.0)
        L = L * wa + wb
        O = O * wa + o_recv[src].astype(F32) * wb
        M = top
    ag[mine] = (O / L).astype(BF16)

    partner = mine + 1 - 2 * lax.rem(mine, 2)

    def ag_copy(slot, to, sem):
        return pltpu.make_async_remote_copy(
            src_ref=ag.at[slot], dst_ref=ag.at[slot], send_sem=sem, recv_sem=agr_sem.at[slot],
            device_id={"seq": to * k + sub}, device_id_type=MESH)

    others = [lax.rem(mine + 2 * j, pairs) for j in range(1, pairs // 2)]
    order = sorted(range(len(others)), key=lambda j: abs(j + 1 - pairs / 4))
    for j in order:
        ag_copy(mine, others[j], ags_sem.at[others[j]]).start()
    ag_copy(mine, partner, ags_sem.at[partner]).start()

    g24 = 2 * rounds * R

    def pair_source(r):
        g, q = r // g24, r % g24
        kind, q = q // (rounds * R), q % (rounds * R)
        return kind * rows1 + (q // R) * (group * R) + g * R + q % R

    perm = onehot(rows, rows, pair_source)

    def place(slot):
        b = lax.div(slot, heads)
        h = lax.rem(slot, heads)
        y = jnp.dot(perm, ag[slot], preferred_element_type=F32)
        at = pl.ds(pl.multiple_of(b * g24, g24), g24)
        for g in range(group):
            amat[h, at, g * HD:(g + 1) * HD] = y[g * g24:(g + 1) * g24]

    place(mine)
    far = [others[j] for j in reversed(range(len(others)))]
    for q in far:
        ag_copy(q, partner, agf_sem.at[q]).wait_recv()
        ag_copy(q, partner, agf_sem.at[q]).start()
        place(q)
    for q in [partner] + [lax.rem(partner + 2 * j, pairs) for j in range(1, pairs // 2)]:
        ag_copy(q, partner, agf_sem.at[q]).wait_recv()
        place(q)

    tokens = batch * g24

    def out_source(r):
        t, q = r // (2 * batch * R), r % (2 * batch * R)
        kind, q = q // (batch * R), q % (batch * R)
        return (q // R) * g24 + kind * (rounds * R) + t * R + q % R

    operm = onehot(tokens, tokens, out_source)
    lhs = [
        jnp.dot(operm, amat[h].astype(BF16), preferred_element_type=F32).astype(BF16)
        for h in range(heads)
    ]
    cp_wout.wait()
    depth = group * HD

    def project(cols):
        acc = jnp.dot(lhs[0], wout[0:depth, cols], preferred_element_type=F32)
        for h in range(1, heads):
            acc += jnp.dot(lhs[h], wout[h * depth:(h + 1) * depth, cols], preferred_element_type=F32)
        return acc

    def rs_copy(src, to, slot):
        return pltpu.make_async_remote_copy(
            src_ref=rs_send.at[src], dst_ref=rs_recv.at[slot], send_sem=rss_sem.at[to],
            recv_sem=rsr_sem.at[slot], device_id={"tp": to}, device_id_type=MESH)

    def fin_copy(to, slot):
        return pltpu.make_async_remote_copy(
            src_ref=fin.at[slot], dst_ref=fin.at[slot], send_sem=fs_sem.at[to],
            recv_sem=ffr_sem.at[slot], device_id={"tp": to}, device_id_type=MESH)

    peers = [lax.rem(tpi + j, tp) for j in range(1, tp)]
    if split_cols:
        width = rs_send.shape[2]
        chunk = lambda c: pl.ds(pl.multiple_of(c * width, LANES), width)
        for c in peers:
            rs_send[c] = project(chunk(c)).astype(BF16)
            rs_copy(c, c, tpi).start()
        own = project(chunk(tpi))
        for c in peers:
            rs_copy(c, c, c).wait_recv()
            own = own + rs_recv[c].astype(F32)
        fin[tpi] = own.astype(BF16)
        for c in peers:
            fin_copy(c, tpi).start()
        for c in peers:
            fin_copy(c, c).wait_recv()
        for c in range(tp):
            out_ref[:, c * width:(c + 1) * width] = fin[c]
        for c in peers:
            fin_copy(c, tpi).wait_send()
            rs_copy(c, c, tpi).wait_send()
    else:
        own = project(slice(None))
        rs_send[0] = own.astype(BF16)
        for c in peers:
            rs_copy(0, c, tpi).start()
        for c in peers:
            rs_copy(0, c, c).wait_recv()
        rs_recv[tpi] = rs_send[0]
        total = rs_recv[0].astype(F32)
        for c in range(1, tp):
            total = total + rs_recv[c].astype(F32)
        out_ref[...] = total.astype(BF16)
        for c in peers:
            rs_copy(0, c, tpi).wait_send()

    for j in range(1, n):
        dst = lax.rem(me + j, n)
        fresh_copy(dst, me).wait_send()
        o_copy(0, dst, me, o_send.at[0]).wait_send()
        s_copy(0, dst, me, st_send.at[0]).wait_send()
    for q in others:
        ag_copy(mine, q, ags_sem.at[q]).wait_send()
        ag_copy(q, partner, agf_sem.at[q]).wait_send()
    ag_copy(mine, partner, ags_sem.at[partner]).wait_send()


def per_device(n, tp, hidden_new, w_kv, w_out, queries_draft, queries_verify, keys_cache,
               values_cache, key_levels, value_levels, key_scales, value_scales, lengths, accepted):
    batch, heads, S, HD = keys_cache.shape
    rounds = hidden_new.shape[0]
    R = hidden_new.shape[1] // batch
    group = queries_draft.shape[3] // R
    pairs = batch * heads
    feats = hidden_new.shape[2]
    cols = w_out.shape[1]
    rows = 2 * rounds * group * R
    tokens = 2 * rounds * batch * R
    fpad = -(-rounds * R // 16) * 16
    pad_rows = -(-rows // LANES) * LANES
    split_cols = cols % (tp * LANES) == 0
    width = cols // tp if split_cols else cols
    cfg = (n, tp, batch, heads, rounds, R, group, S, HD, split_cols)
    scales = jnp.concatenate(
        [key_scales.reshape(pairs, S // LANES, LANES), value_scales.reshape(pairs, S // LANES, LANES)], axis=1)
    vm = pl.BlockSpec(memory_space=pltpu.VMEM)
    sm = pl.BlockSpec(memory_space=pltpu.SMEM)
    hb = pl.BlockSpec(memory_space=pl.ANY)
    dma = lambda *shape: pltpu.SemaphoreType.DMA(shape)
    out = pl.pallas_call(
        functools.partial(kernel, cfg),
        out_shape=jax.ShapeDtypeStruct((tokens, cols), BF16),
        in_specs=[sm, sm, vm, vm, vm, vm, hb, hb, hb, hb, hb, hb],
        out_specs=vm,
        scratch_shapes=[
            pltpu.VMEM((feats, heads * 2 * HD), BF16),
            pltpu.VMEM(w_out.shape, BF16),
            pltpu.VMEM((pairs, S, HD), BF16),
            pltpu.VMEM((pairs, S, HD), BF16),
            pltpu.VMEM((pairs, S, HD), BF16),
            pltpu.VMEM((pairs, S, HD), BF16),
            pltpu.VMEM((S, HD), BF16),
            pltpu.VMEM((S, HD), BF16),
            pltpu.VMEM((8, LANES), F32),
            pltpu.VMEM((pairs, fpad, 2 * HD), F32),
            pltpu.VMEM((n, fpad, 2 * HD), F32),
            pltpu.VMEM((pairs, rows, HD), BF16),
            pltpu.VMEM((n, rows, HD), BF16),
            pltpu.VMEM((pairs, 8, pad_rows), F32),
            pltpu.VMEM((n, 8, pad_rows), F32),
            pltpu.VMEM((pairs, rows, HD), BF16),
            pltpu.VMEM((heads, batch * 2 * rounds * R, group * HD), F32),
            pltpu.VMEM((tp, tokens, width), BF16),
            pltpu.VMEM((tp, tokens, width), BF16),
            pltpu.VMEM((tp, tokens, width), BF16),
            dma(2), dma(4, pairs), dma(n), dma(n), dma(n), dma(n), dma(n), dma(n),
            dma(pairs), dma(pairs), dma(pairs), dma(tp), dma(tp), dma(tp), dma(tp),
        ],
        compiler_params=pltpu.CompilerParams(
            collective_id=0, has_side_effects=True, vmem_limit_bytes=60 * 1024 * 1024),
    )(lengths, accepted, hidden_new.reshape(rounds * batch * R, feats), scales, queries_draft,
      queries_verify, w_kv.reshape(feats, heads * 2 * HD), w_out, keys_cache, values_cache,
      key_levels, value_levels)
    return out.reshape(rounds, 2, batch * R, cols)


def solution(mesh):
    return jax.shard_map(
        functools.partial(per_device, mesh.shape["seq"], mesh.shape["tp"]),
        mesh=mesh,
        in_specs=(
            P(None, None, "seq"),
            P("seq", "tp", None),
            P("tp", "seq"),
            P(None, None, "tp", None, None),
            P(None, None, "tp", None, None),
            P(None, "tp", "seq", None),
            P(None, "tp", "seq", None),
            P(None, "tp", "seq", None),
            P(None, "tp", "seq", None),
            P(None, "tp", "seq"),
            P(None, "tp", "seq"),
            P(),
            P(),
        ),
        out_specs=P(None, None, None, "seq"),
        check_vma=False,
    )
```

```python
import functools
import math

import jax
import jax.numpy as jnp
from jax import lax
from jax.experimental import pallas as pl
from jax.experimental.pallas import tpu as pltpu
from jax.sharding import PartitionSpec as P

NEG = -1e30
LANES = 128
F32 = jnp.float32
BF16 = jnp.bfloat16


def onehot(rows, cols, source):
    r = lax.broadcasted_iota(jnp.int32, (rows, cols), 0)
    c = lax.broadcasted_iota(jnp.int32, (rows, cols), 1)
    return (source(r) == c).astype(F32).astype(BF16)


def kernel(cfg, *refs):
    (len_s, acc_s, hid_v, ks_v, vs_v, qd_v, qv_v, wkv_h, wout_h, k_h, v_h, kl_h, vl_h, out_ref,
     wkv, wout, kc, vc, kl, vl, lowk, lowv, scores,
     fr_send, fr_recv, o_send, o_recv, st_send, st_recv, ag, amat, rs_send, rs_recv, fin,
     in_sem, kv_sem, frs_sem, frr_sem, os_sem, or_sem, ss_sem, sr_sem,
     ags_sem, agf_sem, agr_sem, rss_sem, rsr_sem, fs_sem, ffr_sem) = refs
    n, tp, batch, heads, rounds, R, group, S, HD, split_cols = cfg
    pairs = batch * heads
    k = n // pairs
    rows1 = rounds * group * R
    rows = 2 * rows1
    fpad = fr_send.shape[1]
    pad_rows = st_send.shape[2]
    me = lax.axis_index("seq")
    tpi = lax.axis_index("tp")
    mine = lax.div(me, k)
    sub = lax.rem(me, k)
    MESH = pl.DeviceIdType.MESH

    cp_wkv = pltpu.make_async_copy(wkv_h, wkv, in_sem.at[0])
    cp_wkv.start()
    cp_wout = pltpu.make_async_copy(wout_h, wout, in_sem.at[1])

    def cache_copies(p):
        b = lax.div(p, heads)
        h = lax.rem(p, heads)
        return [
            pltpu.make_async_copy(src.at[b, h], dst.at[p], kv_sem.at[j, p])
            for j, (src, dst) in enumerate(((kl_h, kl), (k_h, kc), (vl_h, vl), (v_h, vc)))
        ]

    for step in range(1, pairs + 1):
        for c in cache_copies(lax.rem(mine + step, pairs)):
            c.start()
    cp_wout.start()

    barrier = pltpu.get_barrier_semaphore()
    for j in range(1, n):
        pl.semaphore_signal(barrier, inc=1, device_id={"seq": lax.rem(me + j, n)}, device_id_type=MESH)
    for j in range(1, tp):
        pl.semaphore_signal(barrier, inc=1, device_id={"tp": lax.rem(tpi + j, tp)}, device_id_type=MESH)

    tok = rounds * batch * R

    def fresh_source(r):
        b, q = r // fpad, r % fpad
        return jnp.where(q < rounds * R, (q // R) * (batch * R) + b * R + q % R, tok)

    hid = jnp.dot(onehot(batch * fpad, tok, fresh_source), hid_v[...], preferred_element_type=F32).astype(BF16)
    cp_wkv.wait()
    partial = jnp.concatenate(
        [jnp.dot(hid, wkv[:, h, :], preferred_element_type=F32) for h in range(heads)], axis=1)
    for p in range(pairs):
        b, h = p // heads, p % heads
        fr_send[p] = partial[b * fpad:(b + 1) * fpad, h * 2 * HD:(h + 1) * 2 * HD]
    pl.semaphore_wait(barrier, n - 1 + tp - 1)

    def fresh_copy(dst, slot):
        return pltpu.make_async_remote_copy(
            src_ref=fr_send.at[lax.div(dst, k)], dst_ref=fr_recv.at[slot],
            send_sem=frs_sem.at[dst], recv_sem=frr_sem.at[slot],
            device_id={"seq": dst}, device_id_type=MESH)

    for j in range(1, n):
        fresh_copy(lax.rem(me + j, n), me).start()
    fr_recv[me] = fr_send[mine]

    factor = (1.0 / math.sqrt(HD)) * math.log2(math.e)
    eye = (lax.broadcasted_iota(jnp.int32, (LANES, LANES), 0)
           == lax.broadcasted_iota(jnp.int32, (LANES, LANES), 1))

    def to_row(col):
        parts = []
        for c in range(pad_rows // LANES):
            lo, hi = c * LANES, min((c + 1) * LANES, rows)
            piece = jnp.where(eye[: hi - lo], col[lo:hi], 0.0)
            parts.append(jnp.sum(piece, axis=0, keepdims=True))
        return jnp.concatenate(parts, axis=1)

    def to_col(row):
        parts = []
        for c in range(pad_rows // LANES):
            lo, hi = c * LANES, min((c + 1) * LANES, rows)
            piece = jnp.where(eye[: hi - lo], row[:, lo:lo + LANES], 0.0)
            parts.append(jnp.sum(piece, axis=1, keepdims=True))
        return jnp.concatenate(parts, axis=0)

    def one_kind(q, keys, values, usable):
        s = lax.dot_general(q, keys, (((1,), (1,)), ((), ())), preferred_element_type=F32)
        s = jnp.where(usable, s, NEG)
        m = jnp.max(s, axis=1, keepdims=True) * factor
        w = jnp.exp2(s * factor - m).astype(BF16)
        both = jnp.dot(w, jnp.concatenate([values, jnp.ones(values.shape, BF16)], axis=1), preferred_element_type=F32)
        return m, both[:, HD:HD + 1], both[:, :HD]

    def o_copy(p, dst, slot, src):
        return pltpu.make_async_remote_copy(
            src_ref=src, dst_ref=o_recv.at[slot], send_sem=os_sem.at[dst], recv_sem=or_sem.at[slot],
            device_id={"seq": dst}, device_id_type=MESH)

    def s_copy(p, dst, slot, src):
        return pltpu.make_async_remote_copy(
            src_ref=src, dst_ref=st_recv.at[slot], send_sem=ss_sem.at[dst], recv_sem=sr_sem.at[slot],
            device_id={"seq": dst}, device_id_type=MESH)

    def pair_part(p, o_dst, st_dst):
        b = lax.div(p, heads)
        h = lax.rem(p, heads)
        for c in cache_copies(p):
            c.wait()
        count = len_s[b] - me * S

        def some(span):
            chunks = span // LANES
            kr, vr = (jnp.where(h == 0, r[b, 0:1, :span], r[b, heads - 1:heads, :span]) for r in (ks_v, vs_v))
            cut = [x[:, c * LANES:(c + 1) * LANES] for x in (kr, vr) for c in range(chunks)]
            cut += [cut[0]] * (-len(cut) % 8)
            scales = jnp.concatenate(cut, axis=0).T
            for c in range(chunks):
                sl = slice(c * LANES, (c + 1) * LANES)
                lowk[sl] = (kl[p, sl].astype(F32) * scales[:, c:c + 1]).astype(BF16)
                lowv[sl] = (vl[p, sl].astype(F32) * scales[:, chunks + c:chunks + c + 1]).astype(BF16)
            usable = lax.broadcasted_iota(jnp.int32, (1, span), 1) < count
            al = slice(0, span)
            parts = [
                one_kind(qd_v[:, b, h].reshape(rows1, HD), lowk[al], lowv[al], usable),
                one_kind(qv_v[:, b, h].reshape(rows1, HD), kc[p, al], vc[p, al], usable),
            ]
            lses = []
            for j, (m, l, o) in enumerate(parts):
                o_dst[j * rows1:(j + 1) * rows1] = (o / l).astype(BF16)
                lses.append(jnp.where(jnp.full(m.shape, count) > 0, m + jnp.log2(l), NEG))
            st_dst[...] = jnp.broadcast_to(to_row(jnp.concatenate(lses, axis=0)), st_dst.shape)

        some(S)

    @pl.loop(1, pairs)
    def _(step):
        p = lax.rem(mine + step, pairs)
        pair_part(p, o_send.at[p], st_send.at[p])
        for e in range(k):
            dst = p * k + lax.rem(sub + e, k)
            o_copy(p, dst, me, o_send.at[p]).start()
            s_copy(p, dst, me, st_send.at[p]).start()

    pair_part(mine, o_recv.at[me], st_recv.at[me])
    for e in range(1, k):
        dst = mine * k + lax.rem(sub + e, k)
        o_copy(mine, dst, me, o_recv.at[me]).start()
        s_copy(mine, dst, me, st_recv.at[me]).start()

    for j in range(1, n):
        fresh_copy(lax.rem(me + j, n), lax.rem(me + j, n)).wait_recv()
    total = fr_recv[0]
    for j in range(1, n):
        total = total + fr_recv[j]
    new_k = total[:, :HD].astype(BF16)
    new_v = total[:, HD:].astype(BF16)
    bm = lax.div(mine, heads)
    hm = lax.rem(mine, heads)
    r_id = lax.broadcasted_iota(jnp.int32, (rows1, fpad), 0)
    c_id = lax.broadcasted_iota(jnp.int32, (rows1, fpad), 1)
    turn, i_q = r_id // (group * R), r_id % R
    c_turn, c_j = c_id // R, c_id % R
    limit = jnp.zeros((rows1, fpad), jnp.int32)
    for t in range(rounds - 1):
        limit = jnp.where(c_turn == t, acc_s[t, bm], limit)
    see = ((c_turn < turn) & (c_j < limit)) | ((c_turn == turn) & (c_j <= i_q))
    dpart = one_kind(qd_v[:, bm, hm].reshape(rows1, HD), new_k, new_v, see)
    vpart = one_kind(qv_v[:, bm, hm].reshape(rows1, HD), new_k, new_v, see)
    M, L, O = (jnp.concatenate([a, b], axis=0) for a, b in zip(dpart, vpart))
    for j in range(n):
        src = lax.rem(me + j, n)
        if j:
            o_copy(mine, src, src, o_send.at[0]).wait_recv()
            s_copy(mine, src, src, st_send.at[0]).wait_recv()
        lse = to_col(st_recv[src][0:1])
        top = jnp.maximum(M, lse)
        wa = jnp.exp2(M - top)
        wb = jnp.where(lse > 0.5 * NEG, jnp.exp2(lse - top), 0.0)
        L = L * wa + wb
        O = O * wa + o_recv[src].astype(F32) * wb
        M = top
    ag[mine] = (O / L).astype(BF16)

    partner = mine + 1 - 2 * lax.rem(mine, 2)

    def ag_copy(slot, to, sem):
        return pltpu.make_async_remote_copy(
            src_ref=ag.at[slot], dst_ref=ag.at[slot], send_sem=sem, recv_sem=agr_sem.at[slot],
            device_id={"seq": to * k + sub}, device_id_type=MESH)

    others = [lax.rem(mine + 2 * j, pairs) for j in range(1, pairs // 2)]
    order = sorted(range(len(others)), key=lambda j: abs(j + 1 - pairs / 4))
    for j in order:
        ag_copy(mine, others[j], ags_sem.at[others[j]]).start()
    ag_copy(mine, partner, ags_sem.at[partner]).start()

    g24 = 2 * rounds * R

    def pair_source(r):
        g, q = r // g24, r % g24
        kind, q = q // (rounds * R), q % (rounds * R)
        return kind * rows1 + (q // R) * (group * R) + g * R + q % R

    perm = onehot(rows, rows, pair_source)

    def place(slot):
        b = lax.div(slot, heads)
        h = lax.rem(slot, heads)
        y = jnp.dot(perm, ag[slot], preferred_element_type=F32)
        at = pl.ds(pl.multiple_of(b * g24, g24), g24)
        for g in range(group):
            amat[h, at, g * HD:(g + 1) * HD] = y[g * g24:(g + 1) * g24]

    far = [others[j] for j in reversed(range(len(others)))]
    for q in far:
        ag_copy(q, partner, agf_sem.at[q]).wait_recv()
        ag_copy(q, partner, agf_sem.at[q]).start()
    place(mine)
    for q in far:
        place(q)
    for q in [partner] + [lax.rem(partner + 2 * j, pairs) for j in range(1, pairs // 2)]:
        ag_copy(q, partner, agf_sem.at[q]).wait_recv()
        place(q)

    tokens = batch * g24

    def out_source(r):
        t, q = r // (2 * batch * R), r % (2 * batch * R)
        kind, q = q // (batch * R), q % (batch * R)
        return (q // R) * g24 + kind * (rounds * R) + t * R + q % R

    operm = onehot(tokens, tokens, out_source)
    lhs = [
        jnp.dot(operm, amat[h].astype(BF16), preferred_element_type=F32).astype(BF16)
        for h in range(heads)
    ]
    cp_wout.wait()
    depth = group * HD

    def project(cols):
        acc = jnp.dot(lhs[0], wout[0:depth, cols], preferred_element_type=F32)
        for h in range(1, heads):
            acc += jnp.dot(lhs[h], wout[h * depth:(h + 1) * depth, cols], preferred_element_type=F32)
        return acc

    def rs_copy(src, to, slot):
        return pltpu.make_async_remote_copy(
            src_ref=rs_send.at[src], dst_ref=rs_recv.at[slot], send_sem=rss_sem.at[to],
            recv_sem=rsr_sem.at[slot], device_id={"tp": to}, device_id_type=MESH)

    def fin_copy(to, slot):
        return pltpu.make_async_remote_copy(
            src_ref=fin.at[slot], dst_ref=fin.at[slot], send_sem=fs_sem.at[to],
            recv_sem=ffr_sem.at[slot], device_id={"tp": to}, device_id_type=MESH)

    peers = [lax.rem(tpi + j, tp) for j in range(1, tp)]
    if split_cols:
        width = rs_send.shape[2]
        chunk = lambda c: pl.ds(pl.multiple_of(c * width, LANES), width)
        for c in peers:
            rs_send[c] = project(chunk(c)).astype(BF16)
            rs_copy(c, c, tpi).start()
        own = project(chunk(tpi))
        for c in peers:
            rs_copy(c, c, c).wait_recv()
            own = own + rs_recv[c].astype(F32)
        fin[tpi] = own.astype(BF16)
        for c in peers:
            fin_copy(c, tpi).start()
        for c in peers:
            fin_copy(c, c).wait_recv()
        for c in range(tp):
            out_ref[:, c * width:(c + 1) * width] = fin[c]
        for c in peers:
            fin_copy(c, tpi).wait_send()
            rs_copy(c, c, tpi).wait_send()
    else:
        own = project(slice(None))
        rs_send[0] = own.astype(BF16)
        for c in peers:
            rs_copy(0, c, tpi).start()
        for c in peers:
            rs_copy(0, c, c).wait_recv()
        rs_recv[tpi] = rs_send[0]
        total = rs_recv[0].astype(F32)
        for c in range(1, tp):
            total = total + rs_recv[c].astype(F32)
        out_ref[...] = total.astype(BF16)
        for c in peers:
            rs_copy(0, c, tpi).wait_send()

    for j in range(1, n):
        dst = lax.rem(me + j, n)
        fresh_copy(dst, me).wait_send()
        o_copy(0, dst, me, o_send.at[0]).wait_send()
        s_copy(0, dst, me, st_send.at[0]).wait_send()
    for q in others:
        ag_copy(mine, q, ags_sem.at[q]).wait_send()
        ag_copy(q, partner, agf_sem.at[q]).wait_send()
    ag_copy(mine, partner, ags_sem.at[partner]).wait_send()


def per_device(n, tp, hidden_new, w_kv, w_out, queries_draft, queries_verify, keys_cache,
               values_cache, key_levels, value_levels, key_scales, value_scales, lengths, accepted):
    batch, heads, S, HD = keys_cache.shape
    rounds = hidden_new.shape[0]
    R = hidden_new.shape[1] // batch
    group = queries_draft.shape[3] // R
    pairs = batch * heads
    feats = hidden_new.shape[2]
    cols = w_out.shape[1]
    rows = 2 * rounds * group * R
    tokens = 2 * rounds * batch * R
    fpad = -(-rounds * R // 16) * 16
    pad_rows = -(-rows // LANES) * LANES
    split_cols = cols % (tp * LANES) == 0
    width = cols // tp if split_cols else cols
    cfg = (n, tp, batch, heads, rounds, R, group, S, HD, split_cols)
    vm = pl.BlockSpec(memory_space=pltpu.VMEM)
    sm = pl.BlockSpec(memory_space=pltpu.SMEM)
    hb = pl.BlockSpec(memory_space=pl.ANY)
    dma = lambda *shape: pltpu.SemaphoreType.DMA(shape)
    out = pl.pallas_call(
        functools.partial(kernel, cfg),
        out_shape=jax.ShapeDtypeStruct((tokens, cols), BF16),
        in_specs=[sm, sm, vm, vm, vm, vm, vm, hb, hb, hb, hb, hb, hb],
        out_specs=vm,
        scratch_shapes=[
            pltpu.VMEM(w_kv.shape, BF16),
            pltpu.VMEM(w_out.shape, BF16),
            pltpu.VMEM((pairs, S, HD), BF16),
            pltpu.VMEM((pairs, S, HD), BF16),
            pltpu.VMEM((pairs, S, HD), BF16),
            pltpu.VMEM((pairs, S, HD), BF16),
            pltpu.VMEM((S, HD), BF16),
            pltpu.VMEM((S, HD), BF16),
            pltpu.VMEM((8, LANES), F32),
            pltpu.VMEM((pairs, fpad, 2 * HD), F32),
            pltpu.VMEM((n, fpad, 2 * HD), F32),
            pltpu.VMEM((pairs, rows, HD), BF16),
            pltpu.VMEM((n, rows, HD), BF16),
            pltpu.VMEM((pairs, 8, pad_rows), F32),
            pltpu.VMEM((n, 8, pad_rows), F32),
            pltpu.VMEM((pairs, rows, HD), BF16),
            pltpu.VMEM((heads, batch * 2 * rounds * R, group * HD), F32),
            pltpu.VMEM((tp, tokens, width), BF16),
            pltpu.VMEM((tp, tokens, width), BF16),
            pltpu.VMEM((tp, tokens, width), BF16),
            dma(2), dma(4, pairs), dma(n), dma(n), dma(n), dma(n), dma(n), dma(n),
            dma(pairs), dma(pairs), dma(pairs), dma(tp), dma(tp), dma(tp), dma(tp),
        ],
        compiler_params=pltpu.CompilerParams(
            collective_id=0, has_side_effects=True, vmem_limit_bytes=60 * 1024 * 1024),
    )(lengths, accepted, hidden_new.reshape(rounds * batch * R, feats), key_scales, value_scales, queries_draft,
      queries_verify, w_kv, w_out, keys_cache, values_cache,
      key_levels, value_levels)
    return out.reshape(rounds, 2, batch * R, cols)


def solution(mesh):
    return jax.shard_map(
        functools.partial(per_device, mesh.shape["seq"], mesh.shape["tp"]),
        mesh=mesh,
        in_specs=(
            P(None, None, "seq"),
            P("seq", "tp", None),
            P("tp", "seq"),
            P(None, None, "tp", None, None),
            P(None, None, "tp", None, None),
            P(None, "tp", "seq", None),
            P(None, "tp", "seq", None),
            P(None, "tp", "seq", None),
            P(None, "tp", "seq", None),
            P(None, "tp", "seq"),
            P(None, "tp", "seq"),
            P(),
            P(),
        ),
        out_specs=P(None, None, None, "seq"),
        check_vma=False,
    )
```
